32 devices in a mesh: dp: 4 (over z), ctx: 8 (over y, x, core).
Axes of the slice: x: 2, y: 2, z: 4, core: 2. Of those that a mesh axis runs over, the one named last changes fastest.
Arguments:
- queries: bfloat16 [4, 1024, 2048], P('dp', 'ctx'), may hold values from -6 to 6
- keys: bfloat16 [4, 1024, 2048], P('dp', 'ctx'), may hold values from -6 to 6
- values: bfloat16 [4, 1024, 2048], P('dp', 'ctx'), may hold values from -6 to 6
- out_grad: bfloat16 [4, 1024, 2048], P('dp', 'ctx'), may hold values from -96 to 96
- feature_weight: bfloat16 [16, 128, 128], replicated, may hold values from -0.5 to 0.5
- doc_lengths: int32 [4, 8], P('dp'), may hold values from 1 to 256, 1024 in all within a row
Outputs:
- grad_queries: bfloat16 [4, 1024, 2048], P('dp', 'ctx')
- grad_keys: bfloat16 [4, 1024, 2048], P('dp', 'ctx')
- grad_values: bfloat16 [4, 1024, 2048], P('dp', 'ctx')
- grad_weight: float32 [2048, 128], P(('dp', 'ctx'))
The draws below stay inside these ranges and needn't reach their ends.
Inputs may be any that keep to these rules, and one draw needn't show every extreme that they name: `doc_lengths`: each pack's lengths sum to 1024, and the longest document of each pack has exactly 256 tokens.
All inputs are finite; a program needn't handle non-finite values.
Results may differ from the reference program's by a relative error of at most 0.0015.
Values sent between devices are 32-bit elements; how exact they have to be, the bound alone decides.
No kernel may reach another device: no remote copies, remote signals or barrier semaphores. Data moves between devices by JAX's collectives and lax.ppermute only.
A program may use at most 128 MiB of HBM per device.

```python
import math
import jax
import jax.numpy as jnp
import numpy as np
from jax import lax

HEADS = 16
HEAD_DIM = 128
NDOC = 8
TOKENS = 1024
PACKS = 4


def block_levels(stream_key, dims, pieces, low, top_value):
    loudness = 1.0
    for dim, blocks in pieces:
        draws = jax.random.uniform(jax.random.fold_in(jax.random.fold_in(stream_key, 6), dim), (blocks,), jnp.float32, low / len(pieces), top_value / len(pieces))
        loudness = loudness * jnp.repeat(jnp.exp(draws), dims[dim] // blocks).reshape((-1,) + (1,) * (len(dims) - 1 - dim))
    return loudness


def profile(count, total, bound, skew):
    weights = [(1 << 20) // math.isqrt(grade ** skew) + 1 for grade in range(2, count + 1)]
    surplus, holding = total - bound - (count - 1), [1] * (count - 1)
    while surplus > 0:
        movable = [i for i in range(count - 1) if holding[i] < bound]
        pool, left = sum([weights[i] for i in movable]), surplus
        for i in movable:
            extra = min(bound - holding[i], max(1, left * weights[i] // pool), surplus)
            holding[i] = holding[i] + extra
            surplus = surplus - extra
    return np.array([bound] + holding)


def uneven(key, count, total, reach, skew):
    if count == 2:
        one = jax.random.randint(key, (), max(1, total - reach), min(reach, total - 1) + 1)
        return jnp.stack([one, total - one])
    sizes = jnp.asarray(profile(count, total, reach, skew), jnp.int32)
    pairs = (count - 1) // 2
    giver, taker = sizes[1:1 + 2 * pairs:2], sizes[2:2 + 2 * pairs:2]
    slack = jnp.minimum(giver - 1, reach - taker)
    passed = jax.random.randint(jax.random.fold_in(key, 1), (pairs,), 0, 1 << 20) % (slack + 1)
    sizes = sizes.at[1:1 + 2 * pairs:2].set(giver - passed).at[2:2 + 2 * pairs:2].set(taker + passed)
    return sizes[jax.random.permutation(jax.random.fold_in(key, 2), count)]


def normal_values(key, extent, deviation, bound, split=(), kind=jnp.bfloat16):
    drawn = deviation * jax.random.normal(key, extent, jnp.float32)
    if split:
        drawn = drawn * block_levels(key, extent, split, -0.22, 0.18)
    return jnp.clip(drawn, -bound, bound).astype(kind)


def setup_inputs(seed: int = 0) -> dict:
    streams_of = jax.random.split(jax.random.key(seed), 7)
    queries = normal_values(streams_of[0], (PACKS, TOKENS, HEADS * HEAD_DIM), 1.0, 6.0, ((0, 4), (1, 8)))
    keys = normal_values(streams_of[1], (PACKS, TOKENS, HEADS * HEAD_DIM), 1.0, 6.0, ((0, 4), (1, 8)))
    values = normal_values(streams_of[2], (PACKS, TOKENS, HEADS * HEAD_DIM), 1.0, 6.0, ((0, 4), (1, 8)))
    out_grad = normal_values(streams_of[3], (PACKS, TOKENS, HEADS * HEAD_DIM), 16.0, 96.0, ((0, 4), (1, 8)))
    feature_weight = normal_values(streams_of[4], (HEADS, HEAD_DIM, HEAD_DIM), HEAD_DIM ** -0.5, 0.5)
    doc_lengths = jax.vmap(lambda own: uneven(own, NDOC, TOKENS, TOKENS // 4, 1))(jax.random.split(streams_of[5], PACKS)).reshape((PACKS, NDOC)).astype(jnp.int32)
    return dict(queries=queries, keys=keys, values=values, out_grad=out_grad, feature_weight=feature_weight, doc_lengths=doc_lengths)


def einsum_high(form, *operands):
    return jnp.einsum(form, *operands, precision=lax.Precision.HIGHEST)

def block_scores(feat_q, feat_k, doc_ids):
    count = doc_ids.shape[0]
    causal = jnp.arange(count)[:, None] >= jnp.arange(count)[None, :]
    same_doc = doc_ids[:, None] == doc_ids[None, :]
    keep_mask = (causal & same_doc).astype(jnp.float32)
    scores = einsum_high('thi,shi->hts', feat_q, feat_k) * keep_mask[None]
    return (scores, keep_mask)

def score_gradient(scaled, shift_term, value_heads, keep_mask):
    mixed = einsum_high('the,she->hts', scaled, value_heads) + shift_term.T[:, :, None]
    return mixed * keep_mask[None]

def forward_block(feat_q, feat_k, value_heads, cotangent, doc_ids, state_in, norm_in, carry_doc):
    scores, keep_mask = block_scores(feat_q, feat_k, doc_ids)
    inside = (doc_ids == carry_doc).astype(jnp.float32)[:, None]
    numer = einsum_high('hts,she->the', scores, value_heads) + inside[:, :, None] * einsum_high('thi,hie->the', feat_q, state_in)
    denom = lax.optimization_barrier(jnp.sum(scores, axis=2)).T + inside * einsum_high('thi,hi->th', feat_q, norm_in)
    attn_out = numer / denom[:, :, None]
    scaled = cotangent / denom[:, :, None]
    shift_term = -lax.optimization_barrier(jnp.sum(cotangent * attn_out, axis=2)) / denom
    score_grad = score_gradient(scaled, shift_term, value_heads, keep_mask)
    grad_fq = einsum_high('hts,shi->thi', score_grad, feat_k) + inside[:, :, None] * (einsum_high('hie,the->thi', state_in, scaled) + shift_term[:, :, None] * norm_in[None])
    tail = (doc_ids == doc_ids[-1]).astype(jnp.float32)[:, None, None]
    local_state = einsum_high('thi,the->hie', feat_k * tail, value_heads)
    local_norm = lax.optimization_barrier(jnp.sum(feat_k * tail, axis=0))
    return (scaled, shift_term, grad_fq, local_state, local_norm)

def backward_block(feat_q, feat_k, value_heads, scaled, shift_term, doc_ids, rstate_in, rnorm_in, carry_doc):
    scores, keep_mask = block_scores(feat_q, feat_k, doc_ids)
    score_grad = score_gradient(scaled, shift_term, value_heads, keep_mask)
    inside = (doc_ids == carry_doc).astype(jnp.float32)[:, None, None]
    grad_fk = einsum_high('hts,thi->shi', score_grad, feat_q) + inside * (einsum_high('hie,she->shi', rstate_in, value_heads) + rnorm_in[None])
    grad_value = einsum_high('hts,the->she', scores, scaled) + inside * einsum_high('hie,shi->she', rstate_in, feat_k)
    head_part = (doc_ids == doc_ids[0]).astype(jnp.float32)[:, None, None]
    local_rstate = einsum_high('thi,the->hie', feat_q * head_part, scaled)
    local_rnorm = einsum_high('thi,th->hi', feat_q * head_part, shift_term)
    return (grad_fk, grad_value, local_rstate, local_rnorm)

def reference(queries, keys, values, out_grad, feature_weight, doc_lengths):
    heads = HEADS
    width = HEAD_DIM
    block = math.gcd(TOKENS, 512)
    blocks = TOKENS // block
    weight32 = feature_weight.astype(jnp.float32)

    def one_pack(items):
        query_rows, key_rows, value_rows, grad_rows, lengths = items
        lengths = lengths.astype(jnp.int32)
        starts = (jnp.cumsum(lengths) - lengths).astype(jnp.int32)
        positions = jnp.arange(TOKENS, dtype=jnp.int32)
        doc_ids = (lax.optimization_barrier(jnp.sum((starts[None, :] <= positions[:, None]).astype(jnp.int32), axis=1)) - 1).astype(jnp.int32)
        query_heads = query_rows.reshape(TOKENS, heads, width).astype(jnp.float32)
        key_heads = key_rows.reshape(TOKENS, heads, width).astype(jnp.float32)
        value_heads = value_rows.reshape(TOKENS, heads, width).astype(jnp.float32)
        cotangent = grad_rows.reshape(TOKENS, heads, width).astype(jnp.float32)
        pre_q = einsum_high('thi,hij->thj', query_heads, weight32)
        pre_k = einsum_high('thi,hij->thj', key_heads, weight32)
        feat_q = jax.nn.softplus(pre_q)
        feat_k = jax.nn.softplus(pre_k)

        def split_blocks(array):
            return array.reshape((blocks, block) + array.shape[1:])

        def forward_step(carry, xs):
            state_in, norm_in, carry_doc = carry
            fqb, fkb, vb, gb, db = xs
            scaled, shift_term, grad_fq, local_state, local_norm = forward_block(fqb, fkb, vb, gb, db, state_in, norm_in, carry_doc)
            keep = (carry_doc == db[-1]).astype(jnp.float32)
            return ((local_state + keep * state_in, local_norm + keep * norm_in, db[-1]), (scaled, shift_term, grad_fq))
        init_fwd = (jnp.zeros((heads, width, width), jnp.float32), jnp.zeros((heads, width), jnp.float32), jnp.array(-1, jnp.int32))
        fwd_xs = (split_blocks(feat_q), split_blocks(feat_k), split_blocks(value_heads), split_blocks(cotangent), split_blocks(doc_ids))
        unused, (scaled, shift_term, grad_fq) = lax.scan(forward_step, init_fwd, fwd_xs)

        def backward_step(carry, xs):
            rstate_in, rnorm_in, carry_doc = carry
            fqb, fkb, vb, ab, bb, db = xs
            grad_fk, grad_value, local_rstate, local_rnorm = backward_block(fqb, fkb, vb, ab, bb, db, rstate_in, rnorm_in, carry_doc)
            keep = (carry_doc == db[0]).astype(jnp.float32)
            return ((local_rstate + keep * rstate_in, local_rnorm + keep * rnorm_in, db[0]), (grad_fk, grad_value))
        init_bwd = (jnp.zeros((heads, width, width), jnp.float32), jnp.zeros((heads, width), jnp.float32), jnp.array(-1, jnp.int32))
        bwd_xs = (split_blocks(feat_q), split_blocks(feat_k), split_blocks(value_heads), scaled, shift_term, split_blocks(doc_ids))
        unused_too, (grad_fk, grad_value) = lax.scan(backward_step, init_bwd, bwd_xs, reverse=True)
        grad_fq = grad_fq.reshape(TOKENS, heads, width)
        grad_fk = grad_fk.reshape(TOKENS, heads, width)
        grad_value = grad_value.reshape(TOKENS, heads * width)
        grad_pre_q = grad_fq * jax.nn.sigmoid(pre_q)
        grad_pre_k = grad_fk * jax.nn.sigmoid(pre_k)
        grad_query = einsum_high('thj,hij->thi', grad_pre_q, weight32).reshape(TOKENS, heads * width)
        grad_key = einsum_high('thj,hij->thi', grad_pre_k, weight32).reshape(TOKENS, heads * width)
        weight_term = einsum_high('thi,thj->hij', query_heads, grad_pre_q) + einsum_high('thi,thj->hij', key_heads, grad_pre_k)
        return (grad_query.astype(jnp.bfloat16), grad_key.astype(jnp.bfloat16), grad_value.astype(jnp.bfloat16), weight_term)
    grad_queries, grad_keys, grad_values, weight_terms = lax.map(one_pack, (queries, keys, values, out_grad, doc_lengths))
    factor = 1.0 / math.sqrt(PACKS * TOKENS)
    grad_weight = (lax.optimization_barrier(jnp.sum(weight_terms, axis=0)) * factor).reshape(heads * width, width)
    return (grad_queries, grad_keys, grad_values, grad_weight)
```

```python
import functools
import math

import jax
import jax.numpy as jnp
from jax import lax
from jax.experimental import pallas as pl
from jax.experimental.pallas import tpu as pltpu
from jax.sharding import PartitionSpec as P

F32 = jnp.float32
BF16 = jnp.bfloat16
VM = pl.BlockSpec(memory_space=pltpu.VMEM)
SM = pl.BlockSpec(memory_space=pltpu.SMEM)
NN = (((1,), (0,)), ((), ()))
NT = (((1,), (1,)), ((), ()))
TN = (((0,), (0,)), ((), ()))


def split(x):
    hi = x.astype(BF16)
    return hi, (x - hi.astype(F32)).astype(BF16)


def dot(a, b, dims):
    return lax.dot_general(a, b, dims, preferred_element_type=F32)


def cat(parts, axis):
    return jnp.concatenate(parts, axis=axis)


def dot_wide(a, b, dims):
    ka, kb = dims[0][0][0], dims[0][1][0]
    hi, lo = split(a)
    return dot(cat([hi, lo], ka), cat([b, b], kb), dims)


def dot_full(a, b, dims):
    ka, kb = dims[0][0][0], dims[0][1][0]
    ah, al = split(a)
    bh, bl = split(b)
    return dot(cat([ah, al, ah], ka), cat([bh, bh, bl], kb), dims)


def softplus(x):
    return jnp.maximum(x, 0.0) + jnp.log1p(jnp.exp(-jnp.abs(x)))


def sigmoid(x):
    z = jnp.exp(-jnp.abs(x))
    return jnp.where(x >= 0, 1.0, z) / (1.0 + z)


class Docs:
    def __init__(self, lengths_ref, ndoc, rows):
        self.rows = rows
        self.first = (lax.axis_index("ctx") // 2) * rows
        self.starts = [jnp.int32(0)]
        for d in range(ndoc):
            self.starts.append(self.starts[-1] + lengths_ref[0, d])

    def start_of(self, pos):
        out = jnp.zeros_like(pos)
        for s in self.starts[1:]:
            out = jnp.where(pos >= s, s, out)
        return out

    def along(self, axis, shape):
        return self.first + lax.broadcasted_iota(jnp.int32, shape, axis)

    def keep_t(self):
        shape = (self.rows, self.rows)
        s, t = self.along(0, shape), self.along(1, shape)
        begin = self.start_of(self.along(1, (8, self.rows)))[:1]
        return ((s <= t) & (s >= begin)).astype(F32)

    def inside_row(self):
        return (self.start_of(self.along(1, (8, self.rows))) < self.first).astype(F32)[:1]

    def head_row(self):
        begin = self.start_of(self.along(1, (8, self.rows)))
        return (begin <= self.first).astype(F32)[:1]

    def tail_row(self):
        last = self.start_of(self.first + self.rows - 1 + jnp.int32(0))
        return (self.along(1, (8, self.rows)) >= last).astype(F32)[:1]

    def later_col(self, width):
        after = self.start_of(self.first + self.rows + jnp.int32(0))
        return (self.along(0, (self.rows, width)) >= after).astype(F32)


def my_core():
    return lax.rem(lax.axis_index("ctx"), 2)


def place(ref, h, width):
    return ref[:, pl.ds(pl.multiple_of(h * width, width), width)]


def token_pair(own_ref, got_ref, h, nh, width):
    core = my_core()
    own = own_ref[:, pl.ds(pl.multiple_of((core * nh + h) * width, width), width)].astype(F32)
    got = place(got_ref, h, width)
    first = jnp.where(core == 0, own, got)
    second = jnp.where(core == 0, got, own)
    return cat([first, second], 0).astype(BF16)


def key_kernel(nh, ndoc, len_ref, k_ref, v_ref, kg_ref, vg_ref, w_ref,
               fk_ref, fkt_ref, k2_ref, v2_ref, s_ref, n_ref):
    rows, width = fk_ref.shape[1:]
    tail = Docs(len_ref, ndoc, rows).tail_row()
    core = my_core()

    def body(h, _):
        k = token_pair(k_ref, kg_ref, h, nh, width)
        v = token_pair(v_ref, vg_ref, h, nh, width)
        fk = softplus(dot(k, w_ref[core * nh + h], NN))
        fkt = fk.T
        fk_ref[h] = fk
        fkt_ref[h] = fkt
        k2_ref[h] = k
        v2_ref[h] = v
        masked = fkt * tail
        s_ref[h] = dot_wide(masked, v, NN)
        n_ref[h] = jnp.broadcast_to(jnp.sum(masked, axis=1, keepdims=True), (width, 128)).T[:1]
        return 0

    lax.fori_loop(0, nh, body, 0)


def query_kernel(nh, ndoc, len_ref, q_ref, g_ref, qg_ref, gg_ref, w_ref, fk_ref,
                 fqt_ref, sqt_ref, q2_ref, g2_ref, at_ref, dl_ref):
    rows, width = fk_ref.shape[1:]
    keep = Docs(len_ref, ndoc, rows).keep_t()
    core = my_core()

    def body(h, _):
        q = token_pair(q_ref, qg_ref, h, nh, width)
        q2_ref[h] = q
        g2_ref[h] = token_pair(g_ref, gg_ref, h, nh, width)
        pre = dot(q, w_ref[core * nh + h], NN).T
        fqt = softplus(pre)
        fqt_ref[h] = fqt
        sqt_ref[h] = sigmoid(pre)
        at = dot_full(fk_ref[h], fqt, NN) * keep
        at_ref[h] = at
        dl_ref[h] = jnp.sum(at, axis=0, keepdims=True)
        return 0

    lax.fori_loop(0, nh, body, 0)


def rstate_kernel(nh, ndoc, len_ref, fqt_ref, g2_ref, dl_ref, n_ref, inv_ref, r_ref):
    rows = fqt_ref.shape[2]
    docs = Docs(len_ref, ndoc, rows)
    inside, head = docs.inside_row(), docs.head_row()

    def body(h, _):
        fqt = fqt_ref[h]
        norm = jnp.broadcast_to(n_ref[h], (8, n_ref.shape[2]))
        denom = dl_ref[h] + inside * dot_full(norm, fqt, NN)[:1]
        inv = 1.0 / denom
        inv_ref[h] = inv
        r_ref[h] = dot_wide(fqt * (inv * head), g2_ref[h], NN)
        return 0

    lax.fori_loop(0, nh, body, 0)


def fill_kernel(nh, at_ref, inv_ref, g2_ref, v2_ref, k2_ref, w_ref,
                mt_ref, cl_ref, gv_ref, sk_ref):
    core = my_core()

    def body(h, _):
        at = at_ref[h]
        g, v = g2_ref[h], v2_ref[h]
        mt = dot(v, g, NT)
        mt_ref[h] = mt
        cl_ref[h] = jnp.sum(at * mt, axis=0, keepdims=True)
        gv_ref[h] = dot_wide(at * inv_ref[h], g, NN)
        sk_ref[h] = sigmoid(dot(k2_ref[h], w_ref[core * nh + h], NN))
        return 0

    lax.fori_loop(0, nh, body, 0)


def out_pair(x, own_ref, send_ref, h, width):
    core = my_core()
    half = x.shape[0] // 2
    own = jnp.where(core == 0, x[:half], x[half:])
    other = jnp.where(core == 0, x[half:], x[:half])
    at = pl.ds(pl.multiple_of(h * width, width), width)
    own_ref[:, at] = own.astype(BF16)
    send_ref[:, at] = other


def forward_kernel(nh, ndoc, len_ref, s_ref, n_ref, mt_ref, cl_ref, inv_ref, g2_ref, q2_ref,
                   fqt_ref, sqt_ref, fk_ref, fkt_ref, w_ref,
                   gq_ref, gqs_ref, qt_ref, rn_ref, gfk_ref):
    rows, width = fk_ref.shape[1:]
    docs = Docs(len_ref, ndoc, rows)
    keep, inside, head = docs.keep_t(), docs.inside_row(), docs.head_row()
    core = my_core()

    def body(h, _):
        w = w_ref[core * nh + h]
        fqt, inv = fqt_ref[h], inv_ref[h]
        ut = dot_wide(s_ref[h], g2_ref[h], NT)
        c = (cl_ref[h] + inside * jnp.sum(fqt * ut, axis=0, keepdims=True)) * inv
        shift = -c * inv
        rn_ref[h] = dot_full(jnp.broadcast_to(shift * head, (8, rows)), fqt, NT)[:1]
        pt = (mt_ref[h] - c) * inv * keep
        gfk_ref[h] = dot_full(pt, fqt, NT)
        norm = jnp.broadcast_to(n_ref[h], (width, width)).T
        carried = ut * inv + cat([norm] * (rows // width), 1) * shift
        gfq = dot_full(fkt_ref[h], pt, NN) + inside * carried
        gpq = gfq * sqt_ref[h]
        hi, lo = split(gpq)
        gq = dot(cat([w, w], 1), cat([hi, lo], 0), NN).T
        out_pair(gq, gq_ref, gqs_ref, h, width)
        q = q2_ref[h]
        qt_ref[h] = dot(cat([hi, lo], 1), cat([q, q], 0), NN).T
        return 0

    lax.fori_loop(0, nh, body, 0)


def backward_kernel(nh, ndoc, factor, len_ref, r_ref, rn_ref, gfk_ref, gv0_ref, sk_ref, fk_ref,
                    k2_ref, v2_ref, qt_ref, w_ref,
                    wt_ref, gk_ref, gks_ref, gv_ref, gvs_ref):
    rows, width = fk_ref.shape[1:]
    later = Docs(len_ref, ndoc, rows).later_col(width)
    core = my_core()

    def body(h, _):
        w = w_ref[core * nh + h]
        r = r_ref[h]
        rh, rl = split(r)
        v = v2_ref[h]
        carried = dot(cat([v, v], 1), cat([rh, rl], 1), NT) + rn_ref[h]
        gpk = (gfk_ref[h] + later * carried) * sk_ref[h]
        hi, lo = split(gpk)
        k = k2_ref[h]
        wt_ref[h] = (dot(cat([k, k], 0), cat([hi, lo], 0), TN) + qt_ref[h]) * factor
        out_pair(dot(cat([hi, lo], 1), cat([w, w], 1), NT), gk_ref, gks_ref, h, width)
        fh, fl = split(fk_ref[h])
        gv = gv0_ref[h] + later * dot(cat([fh, fl, fh], 1), cat([rh, rh, rl], 0), NN)
        out_pair(gv, gv_ref, gvs_ref, h, width)
        return 0

    lax.fori_loop(0, nh, body, 0)


def join_kernel(own_ref, got_ref, out_ref):
    core = my_core()
    half = own_ref.shape[1]
    out_ref[:, pl.ds(pl.multiple_of(core * half, half), half)] = own_ref[...]
    out_ref[:, pl.ds(pl.multiple_of((1 - core) * half, half), half)] = got_ref[...].astype(BF16)


def call(kernel, outs, name, smem=0, limit=24 << 20):
    def run(*args):
        return pl.pallas_call(
            kernel,
            out_shape=[jax.ShapeDtypeStruct(s, d) for s, d in outs],
            in_specs=[SM] * smem + [VM] * (len(args) - smem),
            out_specs=[VM] * len(outs),
            compiler_params=pltpu.CompilerParams(vmem_limit_bytes=limit),
            name=name,
        )(*args)

    return run


def shards(queries, keys, values, out_grad, feature_weight, doc_lengths):
    ctx = lax.axis_size("ctx")
    dp = lax.axis_size("dp")
    tok = queries.shape[1]
    heads, width, _ = feature_weight.shape
    ndoc = doc_lengths.shape[1]
    chips = ctx // 2
    nh = heads // 2
    rows = 2 * tok
    here = lax.axis_index("ctx")
    core = here % 2
    chip = here // 2
    longest = ctx * tok // 4
    hops = -(-longest // rows)
    factor = 1.0 / math.sqrt(dp * ctx * tok)

    swap = [(i, i ^ 1) for i in range(ctx)]
    ahead = [(i, i + 2) for i in range(ctx - 2)]
    back = [(i + 2, i) for i in range(ctx - 2)]

    def other_half(x):
        part = lax.dynamic_slice_in_dim(x, (1 - core) * nh * width, nh * width, axis=1)
        return lax.ppermute(part.astype(F32), "ctx", swap)

    q, k, v, g = queries[0], keys[0], values[0], out_grad[0]
    kg, vg = other_half(k), other_half(v)
    qg, gg = other_half(q), other_half(g)
    w = feature_weight

    if hops > 1:
        ends = jnp.cumsum(doc_lengths[0])
        begins = jnp.concatenate([jnp.zeros((1,), jnp.int32), ends])

        def start_of(p):
            return jnp.max(jnp.where(begins <= p, begins, 0))

    def carry(x, forward):
        total = moved = lax.ppermute(x, "ctx", ahead if forward else back)
        for h in range(1, hops):
            moved = lax.ppermute(moved, "ctx", ahead if forward else back)
            if forward:
                gate = start_of(chip * rows) < (chip - h) * rows
            else:
                gate = start_of((chip + 1 + h) * rows) < (chip + 1) * rows
            total = total + jnp.where(gate, moved, 0.0)
        return total

    wide = (nh, rows, width)
    tall = (nh, width, rows)
    square = (nh, rows, rows)
    state = (nh, width, width)
    norm = (nh, 1, width)
    line = (nh, 1, rows)
    half = (tok, nh * width)

    fk, fkt, k2, v2, s_loc, n_loc = call(
        functools.partial(key_kernel, nh, ndoc),
        [(wide, F32), (tall, F32), (wide, BF16), (wide, BF16), (state, F32), (norm, F32)],
        "key", 1,
    )(doc_lengths, k, v, kg, vg, w)
    n_in = carry(n_loc, True)
    s_in = carry(s_loc, True)
    fqt, sqt, q2, g2, at, dl = call(
        functools.partial(query_kernel, nh, ndoc),
        [(tall, F32), (tall, F32), (wide, BF16), (wide, BF16), (square, F32), (line, F32)],
        "query", 1,
    )(doc_lengths, q, g, qg, gg, w, fk)
    inv, r_loc = call(
        functools.partial(rstate_kernel, nh, ndoc), [(line, F32), (state, F32)], "rstate", 1
    )(doc_lengths, fqt, g2, dl, n_in)
    r_in = carry(r_loc, False)
    mt, cl, gv0, sk = call(
        functools.partial(fill_kernel, nh),
        [(square, F32), (line, F32), (wide, F32), (wide, F32)],
        "fill",
    )(at, inv, g2, v2, k2, w)
    gq, gqs, qt, rn, gfk = call(
        functools.partial(forward_kernel, nh, ndoc),
        [(half, BF16), (half, F32), (state, F32), (norm, F32), (wide, F32)],
        "forward", 1,
    )(doc_lengths, s_in, n_in, mt, cl, inv, g2, q2, fqt, sqt, fk, fkt, w)
    rn_in = carry(rn, False)
    gqg = lax.ppermute(gqs, "ctx", swap)
    wt, gk, gks, gv, gvs = call(
        functools.partial(backward_kernel, nh, ndoc, factor),
        [(state, F32), (half, BF16), (half, F32), (half, BF16), (half, F32)],
        "backward", 1,
    )(doc_lengths, r_in, rn_in, gfk, gv0, sk, fk, k2, v2, qt, w)

    each = heads * width // (dp * ctx)
    wt = wt.reshape(dp // 2, chips, 2 * each, width)

    def block(to):
        return lax.dynamic_index_in_dim(wt, to, axis=1, keepdims=False)

    total = block(chip)
    moved = []
    for j in range(1, chips):
        perm = [(i, ((i // 2) ^ j) * 2 + i % 2) for i in range(ctx)]
        moved.append(lax.ppermute(block(chip ^ j), "ctx", perm))
    for part in moved:
        total = total + part
    total = total.reshape(dp, each, width)
    z = lax.axis_index("dp")
    moved = []
    for r in range(dp):
        perm = []
        for zz in range(dp):
            for i in range(ctx):
                to = (i % 2) * (dp // 2) + ((zz ^ r) >> 1)
                perm.append((zz * ctx + i, to * ctx + (i // 2) * 2 + ((zz ^ r) & 1)))
        part = lax.dynamic_index_in_dim(total, z ^ r, axis=0, keepdims=False)
        moved.append(lax.ppermute(part, ("dp", "ctx"), perm))
    grad_weight = functools.reduce(jnp.add, moved)

    gkg = lax.ppermute(gks, "ctx", swap)
    gvg = lax.ppermute(gvs, "ctx", swap)

    def join(own, got):
        return call(join_kernel, [((tok, heads * width), BF16)], "join")(own, got)[0][None]

    return (join(gq, gqg), join(gk, gkg), join(gv, gvg), grad_weight)


def solution(mesh):
    placed = (
        P("dp", "ctx", None),
        P("dp", "ctx", None),
        P("dp", "ctx", None),
        P("dp", "ctx", None),
        P(),
        P("dp", None),
    )
    return jax.shard_map(
        shards,
        mesh=mesh,
        in_specs=placed,
        out_specs=(
            P("dp", "ctx", None),
            P("dp", "ctx", None),
            P("dp", "ctx", None),
            P(("dp", "ctx"), None),
        ),
        check_vma=False,
    )
```

```python
import functools
import math

import jax
import jax.numpy as jnp
from jax import lax
from jax.experimental import pallas as pl
from jax.experimental.pallas import tpu as pltpu
from jax.sharding import PartitionSpec as P

F32 = jnp.float32
BF16 = jnp.bfloat16
SOME = 2
LIMIT = 8 << 20
CAST_LIMIT = 8 << 20
VM = pl.BlockSpec(memory_space=pltpu.VMEM)
SM = pl.BlockSpec(memory_space=pltpu.SMEM)
NN = (((1,), (0,)), ((), ()))
NT = (((1,), (1,)), ((), ()))
TN = (((0,), (0,)), ((), ()))


def split(x):
    hi = x.astype(BF16)
    return hi, (x - hi.astype(F32)).astype(BF16)


def dot(a, b, dims):
    return lax.dot_general(a, b, dims, preferred_element_type=F32)


def cat(parts, axis):
    return jnp.concatenate(parts, axis=axis)


def dot_wide(a, b, dims):
    ka, kb = dims[0][0][0], dims[0][1][0]
    hi, lo = split(a)
    return dot(cat([hi, lo], ka), cat([b, b], kb), dims)


def dot_full(a, b, dims):
    ka, kb = dims[0][0][0], dims[0][1][0]
    ah, al = split(a)
    bh, bl = split(b)
    return dot(cat([ah, al, ah], ka), cat([bh, bh, bl], kb), dims)


def softplus(x):
    z = jnp.exp(-jnp.abs(x))
    small = z * (1.0 - z * (0.5 - z * (1.0 / 3.0 - z * 0.25)))
    return jnp.maximum(x, 0.0) + jnp.where(z < 0.03, small, jnp.log(1.0 + z))


def heads_loop(first, last, load, work, store, some=SOME):
    some = math.gcd(some, last - first)

    def body(p, _):
        hs = [first + p * some + u for u in range(some)]
        outs = [work(*x) for x in [load(h) for h in hs]]
        for h, out in zip(hs, outs):
            store(h, *out)
        return 0

    lax.fori_loop(0, (last - first) // some, body, 0)


class Docs:
    def __init__(self, lengths_ref, ndoc, rows):
        self.rows = rows
        self.first = (lax.axis_index("ctx") // 2) * rows
        self.starts = [jnp.int32(0)]
        for d in range(ndoc):
            self.starts.append(self.starts[-1] + lengths_ref[0, d])

    def start_of(self, pos):
        out = jnp.zeros_like(pos)
        for s in self.starts[1:]:
            out = jnp.where(pos >= s, s, out)
        return out

    def along(self, axis, shape):
        return self.first + lax.broadcasted_iota(jnp.int32, shape, axis)

    def keep_t(self):
        shape = (self.rows, self.rows)
        s, t = self.along(0, shape), self.along(1, shape)
        begin = self.start_of(self.along(1, (8, self.rows)))[:1]
        return ((s <= t) & (s >= begin)).astype(F32)

    def inside_row(self):
        return (self.start_of(self.along(1, (8, self.rows))) < self.first).astype(F32)[:1]

    def head_row(self):
        begin = self.start_of(self.along(1, (8, self.rows)))
        return (begin <= self.first).astype(F32)[:1]

    def tail_row(self):
        last = self.start_of(self.first + self.rows - 1 + jnp.int32(0))
        return (self.along(1, (8, self.rows)) >= last).astype(F32)[:1]

    def later_col(self, width):
        after = self.start_of(self.first + self.rows + jnp.int32(0))
        return (self.along(0, (self.rows, width)) >= after).astype(F32)


def my_core():
    return lax.rem(lax.axis_index("ctx"), 2)


def place(ref, h, width):
    return ref[:, pl.ds(pl.multiple_of(h * width, width), width)]


def token_pair(own_ref, got_ref, h, width):
    core = my_core()
    own = place(own_ref, h, width).astype(F32)
    got = place(got_ref, h, width)
    first = jnp.where(core == 0, own, got)
    second = jnp.where(core == 0, got, own)
    return cat([first, second], 0).astype(BF16)


def cast_kernel(k_ref, v_ref, q_ref, g_ref, w_ref, ko_ref, vo_ref, qo_ref, go_ref,
                ks_ref, vs_ref, qs_ref, gs_ref, wo_ref, bufs, sems):
    core = my_core()
    refs = [k_ref, v_ref, q_ref, g_ref]
    owns = [ko_ref, vo_ref, qo_ref, go_ref]
    sends = [ks_ref, vs_ref, qs_ref, gs_ref]
    half = ko_ref.shape[1]
    nh = wo_ref.shape[0]
    mine = pl.ds(pl.multiple_of(core * half, half), half)
    other = pl.ds(pl.multiple_of((1 - core) * half, half), half)
    out = [pltpu.make_async_copy(r.at[:, other], bufs.at[i], sems.at[i]) for i, r in enumerate(refs)]
    keep = [pltpu.make_async_copy(r.at[:, mine], o, sems.at[4 + i])
            for i, (r, o) in enumerate(zip(refs, owns))]
    keep.append(pltpu.make_async_copy(w_ref.at[pl.ds(core * nh, nh)], wo_ref, sems.at[8]))
    for c in out + keep:
        c.start()
    for i, c in enumerate(out):
        c.wait()
        sends[i][...] = bufs[i].astype(F32)
    for c in keep:
        c.wait()


def mask_kernel(ndoc, len_ref, keep_ref, line_ref, later_ref):
    docs = Docs(len_ref, ndoc, keep_ref.shape[0])
    keep_ref[...] = docs.keep_t()
    line_ref[...] = cat([docs.inside_row(), docs.head_row(), docs.tail_row()] + [docs.tail_row()] * 5, 0)
    later_ref[...] = docs.later_col(later_ref.shape[1])


def key_kernel(nh, k_ref, v_ref, kg_ref, vg_ref, w_ref, line_ref,
               fk_ref, fkt_ref, k2_ref, v2_ref, s1_ref, s2_ref):
    _, width = fk_ref.shape[1:]
    few = nh - s2_ref.shape[0]
    tail = line_ref[2:3]

    def load(h):
        return (token_pair(k_ref, kg_ref, h, width), token_pair(v_ref, vg_ref, h, width),
                w_ref[h])

    def work(k, v, w):
        fk = softplus(dot(k, w, NN))
        fkt = fk.T
        masked = fkt * tail
        norm = jnp.broadcast_to(jnp.sum(masked, axis=1, keepdims=True), (width, 128)).T[:1]
        return fk, fkt, k, v, dot_wide(masked, v, NN), norm

    def store(h, fk, fkt, k, v, s, n):
        fk_ref[h] = fk
        fkt_ref[h] = fkt
        k2_ref[h] = k
        v2_ref[h] = v
        s1_ref[pl.ds(few * width + h, 1)] = n
        return s

    def store1(h, *out):
        s1_ref[pl.ds(pl.multiple_of(h * width, width), width)] = store(h, *out)

    def store2(h, *out):
        s2_ref[h - few] = store(h, *out)

    heads_loop(0, few, load, work, store1)
    heads_loop(few, nh, load, work, store2)


def query_kernel(nh, q_ref, g_ref, qg_ref, gg_ref, w_ref, fk_ref, keep_ref,
                 fqt_ref, pqt_ref, q2_ref, g2_ref, at_ref, dl_ref):
    _, width = fk_ref.shape[1:]

    def load(h):
        return (token_pair(q_ref, qg_ref, h, width), token_pair(g_ref, gg_ref, h, width),
                w_ref[h], fk_ref[h])

    def work(q, g, w, fk):
        pre = dot(q, w, NN).T
        fqt = softplus(pre)
        at = dot_full(fk, fqt, NN) * keep_ref[...]
        return q, g, pre, fqt, at, jnp.sum(at, axis=0, keepdims=True)

    def store(h, q, g, pre, fqt, at, dl):
        q2_ref[h] = q
        g2_ref[h] = g
        pqt_ref[h] = pre
        fqt_ref[h] = fqt
        at_ref[h] = at
        dl_ref[h] = dl

    heads_loop(0, nh, load, work, store)


def rstate_kernel(nh, few, line_ref, fqt_ref, g2_ref, dl_ref, s1_ref, inv_ref, r_ref):
    width = fqt_ref.shape[1]
    inside, head = line_ref[:1], line_ref[1:2]

    def load(h):
        return fqt_ref[h], g2_ref[h], dl_ref[h], s1_ref[pl.ds(few * width + h, 1)]

    def work(fqt, g, dl, n):
        norm = jnp.broadcast_to(n, (8, n.shape[1]))
        denom = dl + inside * dot_full(norm, fqt, NN)[:1]
        inv = 1.0 / denom
        return inv, dot_wide(fqt * (inv * head), g, NN)

    def store(h, inv, r):
        inv_ref[h] = inv
        r_ref[h] = r

    heads_loop(0, nh, load, work, store, 2 * SOME)


def fill_kernel(nh, at_ref, inv_ref, g2_ref, v2_ref, k2_ref, w_ref, fk_ref, pqt_ref, fqt_ref,
                mt_ref, cl_ref, gv_ref, sk_ref, sqt_ref):
    def load(h):
        return (at_ref[h], inv_ref[h], g2_ref[h], v2_ref[h], k2_ref[h], w_ref[h],
                fk_ref[h], pqt_ref[h], fqt_ref[h])

    def work(at, inv, g, v, k, w, fk, pqt, fqt):
        mt = dot(v, g, NT)
        cl = jnp.sum(at * mt, axis=0, keepdims=True)
        gv = dot_wide(at * inv, g, NN)
        return mt, cl, gv, jnp.exp(dot(k, w, NN) - fk), jnp.exp(pqt - fqt)

    def store(h, mt, cl, gv, sk, sqt):
        mt_ref[h] = mt
        cl_ref[h] = cl
        gv_ref[h] = gv
        sk_ref[h] = sk
        sqt_ref[h] = sqt

    heads_loop(0, nh, load, work, store)


def out_pair(x, own_ref, send_ref, h, width):
    core = my_core()
    half = x.shape[0] // 2
    own = jnp.where(core == 0, x[:half], x[half:])
    other = jnp.where(core == 0, x[half:], x[:half])
    at = pl.ds(pl.multiple_of(h * width, width), width)
    own_ref[:, at] = own.astype(BF16)
    send_ref[:, at] = other


def shift_kernel(nh, line_ref, s1_ref, s2_ref, cl_ref, inv_ref, g2_ref, fqt_ref,
                 rn_ref, ut_ref, c_ref):
    rows = fqt_ref.shape[2]
    inside, head = line_ref[:1], line_ref[1:2]

    width = fqt_ref.shape[1]
    few = nh - s2_ref.shape[0]

    def load1(h):
        s = s1_ref[pl.ds(pl.multiple_of(h * width, width), width)]
        return s, cl_ref[h], inv_ref[h], g2_ref[h], fqt_ref[h]

    def load2(h):
        return s2_ref[h - few], cl_ref[h], inv_ref[h], g2_ref[h], fqt_ref[h]

    def work(s, cl, inv, g, fqt):
        ut = dot_wide(s, g, NT)
        c = (cl + inside * jnp.sum(fqt * ut, axis=0, keepdims=True)) * inv
        rn = dot_full(jnp.broadcast_to(-c * inv * head, (8, rows)), fqt, NT)[:1]
        return rn, ut, c

    def store(h, rn, ut, c):
        rn_ref[h] = rn
        ut_ref[h] = ut
        c_ref[h] = c

    heads_loop(0, few, load1, work, store)
    heads_loop(few, nh, load2, work, store)


def forward_kernel(nh, few, line_ref, keep_ref, ut_ref, c_ref, s1_ref, mt_ref, inv_ref, q2_ref,
                   fqt_ref, sqt_ref, fkt_ref, w_ref,
                   gq_ref, gqs_ref, qt_ref, gfk_ref):
    rows, width = gfk_ref.shape[1:]
    inside = line_ref[:1]

    def load(h):
        return (ut_ref[h], c_ref[h], s1_ref[pl.ds(few * width + h, 1)], mt_ref[h], inv_ref[h], q2_ref[h],
                fqt_ref[h], sqt_ref[h], fkt_ref[h], w_ref[h])

    def work(ut, c, n, mt, inv, q, fqt, sqt, fkt, w):
        pt = (mt - c) * inv * keep_ref[...]
        gfk = dot_full(pt, fqt, NT)
        norm = jnp.broadcast_to(n, (width, width)).T
        carried = (ut - cat([norm] * (rows // width), 1) * c) * inv
        gpq = (dot_full(fkt, pt, NN) + inside * carried) * sqt
        hi, lo = split(gpq)
        gq = dot(cat([w, w], 1), cat([hi, lo], 0), NN).T
        qt = dot(cat([hi, lo], 1), cat([q, q], 0), NN).T
        return gq, qt, gfk

    def store(h, gq, qt, gfk):
        out_pair(gq, gq_ref, gqs_ref, h, width)
        qt_ref[h] = qt
        gfk_ref[h] = gfk

    heads_loop(0, nh, load, work, store)


def backward_kernel(nh, factor, later_ref, r_ref, rn_ref, gfk_ref, gv0_ref, sk_ref, fk_ref,
                    k2_ref, v2_ref, qt_ref, w_ref,
                    gk_ref, gks_ref, gv_ref, gvs_ref, *more_refs):
    *plane_refs, wt_ref = more_refs
    _, width = fk_ref.shape[1:]
    low, both, _ = plane_refs[0].shape
    chips = len(plane_refs)
    pieces = width // both

    def load(h):
        return (r_ref[h], rn_ref[h], gfk_ref[h], gv0_ref[h], sk_ref[h], fk_ref[h],
                k2_ref[h], v2_ref[h], qt_ref[h], w_ref[h])

    def work(r, rn, gfk, gv0, sk, fk, k, v, qt, w):
        rh, rl = split(r)
        carried = dot(cat([v, v], 1), cat([rh, rl], 1), NT) + rn
        gpk = (gfk + later_ref[...] * carried) * sk
        hi, lo = split(gpk)
        wt = (dot(cat([k, k], 0), cat([hi, lo], 0), TN) + qt) * factor
        gk = dot(cat([hi, lo], 1), cat([w, w], 1), NT)
        fh, fl = split(fk)
        gv = gv0 + later_ref[...] * dot(cat([fh, fl, fh], 1), cat([rh, rh, rl], 0), NN)
        return wt, gk, gv

    def store(h, wt, gk, gv):
        for p in range(pieces):
            wt_ref[h * pieces + p] = wt[p * both : (p + 1) * both]
        out_pair(gk, gk_ref, gks_ref, h, width)
        out_pair(gv, gv_ref, gvs_ref, h, width)

    heads_loop(0, nh, load, work, store)
    chip = lax.axis_index("ctx") // 2
    for j, ref in enumerate(plane_refs):
        for z in range(low):
            ref[z] = wt_ref[z * chips + (chip ^ j)]


def fold_kernel(bit, parts, *refs):
    ins, outs = refs[:parts], refs[parts:]
    here = bit and bit()
    for i in range(outs[0].shape[0]):
        if bit is None:
            outs[0][i] = functools.reduce(jnp.add, [r[i] for r in ins])
        else:
            a = functools.reduce(jnp.add, [r[2 * i] for r in ins])
            b = functools.reduce(jnp.add, [r[2 * i + 1] for r in ins])
            outs[0][i] = jnp.where(here == 0, a, b)
            outs[1][i] = jnp.where(here == 0, b, a)


def pick_kernel(bit, own_ref, got_ref, keep_ref, send_ref):
    here = bit()
    own, got = own_ref[...], got_ref[...]
    keep_ref[...] = jnp.where(here == 0, own, got)
    send_ref[...] = jnp.where(here == 0, got, own)


def join_kernel(own_ref, got_ref, out_ref):
    core = my_core()
    half = own_ref.shape[1]
    out_ref[:, pl.ds(pl.multiple_of(core * half, half), half)] = own_ref[...]
    out_ref[:, pl.ds(pl.multiple_of((1 - core) * half, half), half)] = got_ref[...].astype(BF16)


def dp_bit(step):
    return (lax.axis_index("dp") // step) % 2


def call(kernel, outs, smem=0, hbm=0, scratch=(), limit=LIMIT):
    def run(*args):
        rest = len(args) - smem - hbm
        return pl.pallas_call(
            kernel,
            out_shape=[jax.ShapeDtypeStruct(s, d) for s, d in outs],
            in_specs=[SM] * smem + [pl.BlockSpec(memory_space=pltpu.HBM)] * hbm + [VM] * rest,
            out_specs=[VM] * len(outs),
            scratch_shapes=list(scratch),
            compiler_params=pltpu.CompilerParams(vmem_limit_bytes=limit),
        )(*args)

    return run


def shards(queries, keys, values, out_grad, feature_weight, doc_lengths):
    ctx = lax.axis_size("ctx")
    dp = lax.axis_size("dp")
    tok = queries.shape[1]
    heads, width, _ = feature_weight.shape
    ndoc = doc_lengths.shape[1]
    chips = ctx // 2
    nh = heads // 2
    rows = 2 * tok
    longest = ctx * tok // 4
    hops = -(-longest // rows)
    factor = 1.0 / math.sqrt(dp * ctx * tok)

    swap = [(i, i ^ 1) for i in range(ctx)]
    ahead = [(i, i + 2) for i in range(ctx - 2)]
    back = [(i + 2, i) for i in range(ctx - 2)]

    q, k, v, g = queries[0], keys[0], values[0], out_grad[0]
    w = feature_weight
    half = (tok, nh * width)

    def swapped(*arrays):
        return [lax.ppermute(x, "ctx", swap) for x in arrays]

    wide = (nh, rows, width)
    tall = (nh, width, rows)
    square = (nh, rows, rows)
    state = (nh, width, width)
    norm = (nh, 1, width)
    line = (nh, 1, rows)

    few = max(1, nh // 4)

    ko, vo, qo, go, ks, vs, qs, gs, w = call(
        cast_kernel, [(half, BF16)] * 4 + [(half, F32)] * 4 + [((nh, width, width), BF16)],
        0, 5, [pltpu.VMEM((4,) + half, BF16), pltpu.SemaphoreType.DMA((9,))], CAST_LIMIT,
    )(*[pltpu.with_memory_space_constraint(x, pltpu.HBM) for x in (k, v, q, g, w)])
    kg, vg = swapped(ks, vs)
    qg, gg = swapped(qs, gs)
    keep, lines, later = call(
        functools.partial(mask_kernel, ndoc),
        [((rows, rows), F32), ((8, rows), F32), ((rows, width), F32)],
        1,
    )(doc_lengths)

    if hops > 1:
        ends = jnp.cumsum(doc_lengths[0])
        begins = jnp.concatenate([jnp.zeros((1,), jnp.int32), ends])

        chip = lax.axis_index("ctx") // 2

        def start_of(p):
            return jnp.max(jnp.where(begins <= p, begins, 0))

    def carry(x, forward):
        total = moved = lax.ppermute(x, "ctx", ahead if forward else back)
        for h in range(1, hops):
            moved = lax.ppermute(moved, "ctx", ahead if forward else back)
            if forward:
                gate = start_of(chip * rows) < (chip - h) * rows
            else:
                gate = start_of((chip + 1 + h) * rows) < (chip + 1) * rows
            total = total + jnp.where(gate, moved, 0.0)
        return total

    fk, fkt, k2, v2, s1, s2 = call(
        functools.partial(key_kernel, nh),
        [(wide, F32), (tall, F32), (wide, BF16), (wide, BF16),
         ((few * width + -(-nh // 8) * 8, width), F32), ((nh - few, width, width), F32)],
    )(ko, vo, kg, vg, w, lines)
    s1 = carry(s1, True)
    s2 = carry(s2, True)
    fqt, pqt, q2, g2, at, dl = call(
        functools.partial(query_kernel, nh),
        [(tall, F32), (tall, F32), (wide, BF16), (wide, BF16), (square, F32), (line, F32)],
    )(qo, go, qg, gg, w, fk, keep)
    inv, r_loc = call(
        functools.partial(rstate_kernel, nh, few), [(line, F32), (state, F32)]
    )(lines, fqt, g2, dl, s1)
    r_in = carry(r_loc, False)
    mt, cl, gv0, sk, sqt = call(
        functools.partial(fill_kernel, nh),
        [(square, F32), (line, F32), (wide, F32), (wide, F32), (tall, F32)],
    )(at, inv, g2, v2, k2, w, fk, pqt, fqt)
    rn, ut, c = call(
        functools.partial(shift_kernel, nh), [(norm, F32), (tall, F32), (line, F32)]
    )(lines, s1, s2, cl, inv, g2, fqt)
    rn_in = carry(rn, False)
    gq, gqs, qt, gfk = call(
        functools.partial(forward_kernel, nh, few),
        [(half, BF16), (half, F32), (state, F32), (wide, F32)],
    )(lines, keep, ut, c, s1, mt, inv, q2, fqt, sqt, fkt, w)

    each = heads * width // (dp * ctx)
    low = dp // 2
    gk, gks, gv, gvs, *planes = call(
        functools.partial(backward_kernel, nh, factor),
        [(half, BF16), (half, F32), (half, BF16), (half, F32)] + [((low, 2 * each, width), F32)] * chips,
        scratch=[pltpu.VMEM((low * chips, 2 * each, width), F32)],
    )(later, r_in, rn_in, gfk, gv0, sk, fk, k2, v2, qt, w)

    def join(own, got):
        return call(join_kernel, [((tok, heads * width), BF16)])(own, got)[0][None]

    moved = []
    for j in range(1, chips):
        perm = [(i, ((i // 2) ^ j) * 2 + i % 2) for i in range(ctx)]
        moved.append(lax.ppermute(planes[j], "ctx", perm))
    gqs, gks, gvs = lax.optimization_barrier((gqs, gks, gvs, planes[0]))[:3]
    gqg, gkg, gvg = swapped(gqs, gks, gvs)
    out_q, out_k, out_v = join(gq, gqg), join(gk, gkg), join(gv, gvg)

    def folded(parts, size, bit):
        return call(
            functools.partial(fold_kernel, bit, len(parts)),
            [(size, F32)] * (1 if bit is None else 2),
        )(*parts)

    parts = [planes[0]] + moved
    left, step = low, 1
    while left > 1:
        left //= 2
        kept, sent = folded(parts, (left, 2 * each, width), functools.partial(dp_bit, step))
        if step == 1:
            sent, out_q, out_k, out_v = lax.optimization_barrier((sent, out_q, out_k, out_v))
        parts = [kept, lax.ppermute(sent, "dp", [(i, i ^ step) for i in range(dp)])]
        step *= 2
    parts = [x.reshape(2, each, width) for x in parts]
    kept, sent = folded(parts, (1, each, width), my_core)
    (got,) = swapped(sent)
    kept, sent = call(
        functools.partial(pick_kernel, lambda: dp_bit(step) ^ my_core()),
        [((1, each, width), F32)] * 2,
    )(kept, got)
    parts = [kept, lax.ppermute(sent, "dp", [(i, i ^ step) for i in range(dp)])]
    (grad_weight,) = folded(parts, (1, each, width), None)
    return (out_q, out_k, out_v, grad_weight[0])


def solution(mesh):
    placed = (
        P("dp", "ctx", None),
        P("dp", "ctx", None),
        P("dp", "ctx", None),
        P("dp", "ctx", None),
        P(),
        P("dp", None),
    )
    return jax.shard_map(
        shards,
        mesh=mesh,
        in_specs=placed,
        out_specs=(
            P("dp", "ctx", None),
            P("dp", "ctx", None),
            P("dp", "ctx", None),
            P(("dp", "ctx"), None),
        ),
        check_vma=False,
    )
```

```python
import functools
import math

import jax
import jax.numpy as jnp
from jax import lax
from jax.experimental import pallas as pl
from jax.experimental.pallas import tpu as pltpu
from jax.sharding import PartitionSpec as P

F32 = jnp.float32
BF16 = jnp.bfloat16
SOME = 8
LIMIT = 8 << 20
VM = pl.BlockSpec(memory_space=pltpu.VMEM)
NN = (((1,), (0,)), ((), ()))
NT = (((1,), (1,)), ((), ()))
TN = (((0,), (0,)), ((), ()))


def split(x):
    hi = x.astype(BF16)
    return hi, (x - hi.astype(F32)).astype(BF16)


def dot(a, b, dims):
    return lax.dot_general(a, b, dims, preferred_element_type=F32)


def cat(parts, axis):
    return jnp.concatenate(parts, axis=axis)


def dot_wide(a, b, dims):
    ka, kb = dims[0][0][0], dims[0][1][0]
    hi, lo = split(a)
    return dot(cat([hi, lo], ka), cat([b, b], kb), dims)


def dot_full(a, b, dims):
    ka, kb = dims[0][0][0], dims[0][1][0]
    ah, al = split(a)
    bh, bl = split(b)
    return dot(cat([ah, al, ah], ka), cat([bh, bh, bl], kb), dims)


def softplus(x):
    z = jnp.exp(-jnp.abs(x))
    small = z * (1.0 - z * (0.5 - z * (1.0 / 3.0 - z * 0.25)))
    return jnp.maximum(x, 0.0) + jnp.where(z < 0.03, small, jnp.log(1.0 + z))


def heads_loop(nh, load, work, store):
    for p in range(0, nh, SOME):
        hs = range(p, min(p + SOME, nh))
        outs = [work(*x) for x in [load(h) for h in hs]]
        for h, out in zip(hs, outs):
            store(h, *out)


class Docs:
    def __init__(self, lengths_ref, ndoc, rows):
        self.rows = rows
        self.first = (lax.axis_index("ctx") // 2) * rows
        self.starts = [jnp.int32(0)]
        for d in range(ndoc):
            self.starts.append(self.starts[-1] + lengths_ref[0, d])

    def start_of(self, pos):
        out = jnp.zeros_like(pos)
        for s in self.starts[1:]:
            out = jnp.where(pos >= s, s, out)
        return out

    def along(self, axis, shape):
        i = lax.broadcasted_iota(jnp.int32, shape, axis)
        half = self.rows // 2
        return self.first + jnp.where(i < half, i + my_core() * half, i - my_core() * half)

    def keep_t(self):
        shape = (self.rows, self.rows)
        s, t = self.along(0, shape), self.along(1, shape)
        begin = self.start_of(self.along(1, (8, self.rows)))[:1]
        return ((s <= t) & (s >= begin)).astype(F32)

    def inside_row(self):
        return (self.start_of(self.along(1, (8, self.rows))) < self.first).astype(F32)[:1]

    def head_row(self):
        begin = self.start_of(self.along(1, (8, self.rows)))
        return (begin <= self.first).astype(F32)[:1]

    def tail_row(self):
        last = self.start_of(self.first + self.rows - 1 + jnp.int32(0))
        return (self.along(1, (8, self.rows)) >= last).astype(F32)[:1]

    def tail_col(self, width):
        last = self.start_of(self.first + self.rows - 1 + jnp.int32(0))
        return (self.along(0, (self.rows, width)) >= last).astype(F32)

    def later_col(self, width):
        after = self.start_of(self.first + self.rows + jnp.int32(0))
        return (self.along(0, (self.rows, width)) >= after).astype(F32)


def my_core():
    return lax.rem(lax.axis_index("ctx"), 2)


def lanes(ref, h, width):
    return ref[:, h * width : (h + 1) * width]


def pair(own_ref, got_ref, h, width):
    return cat([lanes(own_ref, h, width), lanes(got_ref, h, width).astype(BF16)], 0)


def both(own_ref, got_ref, h, axis):
    return cat([own_ref[h], got_ref[h]], axis)


def cast_kernel(ndoc, k_ref, v_ref, q_ref, g_ref, w_ref, len_ref, ko_ref, vo_ref, qo_ref, go_ref,
                ks_ref, vs_ref, qs_ref, gs_ref, wo_ref, keep_ref, line_ref, tail_ref, later_ref,
                bufs, lengths, sems):
    core = my_core()
    refs = [k_ref, v_ref, q_ref, g_ref]
    owns = [ko_ref, vo_ref, qo_ref, go_ref]
    sends = [ks_ref, vs_ref, qs_ref, gs_ref]
    half = ko_ref.shape[1]
    nh = wo_ref.shape[0]
    mine = pl.ds(pl.multiple_of(core * half, half), half)
    other = pl.ds(pl.multiple_of((1 - core) * half, half), half)
    out = [pltpu.make_async_copy(r.at[:, other], bufs.at[i], sems.at[i]) for i, r in enumerate(refs)]
    keep = [pltpu.make_async_copy(r.at[:, mine], o, sems.at[4 + i])
            for i, (r, o) in enumerate(zip(refs, owns))]
    keep.append(pltpu.make_async_copy(w_ref.at[pl.ds(core * nh, nh)], wo_ref, sems.at[8]))
    lens = pltpu.make_async_copy(len_ref, lengths, sems.at[9])
    lens.start()
    for c in out + keep:
        c.start()
    lens.wait()
    docs = Docs(lengths, ndoc, keep_ref.shape[0])
    line_ref[...] = cat([docs.inside_row(), docs.head_row()] + [docs.tail_row()] * 6, 0)
    tail_ref[...] = docs.tail_col(tail_ref.shape[1])
    later_ref[...] = docs.later_col(later_ref.shape[1])
    keep_ref[...] = docs.keep_t()
    for i, c in enumerate(out):
        c.wait()
        sends[i][...] = bufs[i].astype(F32)
    for c in keep:
        c.wait()


def key_half(k, v, w, col, row):
    fk = softplus(dot(k, w, NN))
    fkt = fk.T
    return fk, fkt, dot_wide(fkt * row, v, NN), jnp.sum(fk * col, axis=0, keepdims=True)


def own_key_kernel(nh, k_ref, v_ref, w_ref, line_ref, tail_ref, fk_ref, fkt_ref, s_ref, n_ref):
    rows, width = fk_ref.shape[1:]

    def load(h):
        return (lanes(k_ref, h, width), lanes(v_ref, h, width), w_ref[h],
                tail_ref[:rows], line_ref[2:3, :rows])

    def store(h, fk, fkt, s, n):
        fk_ref[h] = fk
        fkt_ref[h] = fkt
        s_ref[h] = s
        n_ref[h] = n

    heads_loop(nh, load, key_half, store)


def got_key_kernel(nh, k_ref, v_ref, w_ref, line_ref, tail_ref, s_ref, n_ref,
                   fk_ref, fkt_ref, s1_ref, s2_ref):
    rows, width = fk_ref.shape[1:]
    few = nh - s2_ref.shape[0]

    def load(h):
        return (lanes(k_ref, h, width).astype(BF16), lanes(v_ref, h, width).astype(BF16), w_ref[h],
                tail_ref[rows:], line_ref[2:3, rows:])

    def store(h, fk, fkt, s, n):
        fk_ref[h] = fk
        fkt_ref[h] = fkt
        s1_ref[few * width + h : few * width + h + 1] = n + n_ref[h]
        if h < few:
            s1_ref[h * width : (h + 1) * width] = s + s_ref[h]
        else:
            s2_ref[h - few] = s + s_ref[h]

    heads_loop(nh, load, key_half, store)


def query_kernel(nh, q_ref, qg_ref, w_ref, fk_ref, fkg_ref, keep_ref,
                 fqt_ref, pqt_ref, at_ref, dl_ref):
    width = fqt_ref.shape[1]

    def load(h):
        return pair(q_ref, qg_ref, h, width), w_ref[h], both(fk_ref, fkg_ref, h, 0)

    def work(q, w, fk):
        pre = dot(q, w, NN).T
        fqt = softplus(pre)
        at = dot_full(fk, fqt, NN) * keep_ref[...]
        return pre, fqt, at, jnp.sum(at, axis=0, keepdims=True)

    def store(h, pre, fqt, at, dl):
        pqt_ref[h] = pre
        fqt_ref[h] = fqt
        at_ref[h] = at
        dl_ref[h] = dl

    heads_loop(nh, load, work, store)


def rstate_kernel(nh, few, line_ref, fqt_ref, g_ref, gg_ref, dl_ref, s1_ref, inv_ref, r_ref):
    inside, head = line_ref[:1], line_ref[1:2]
    width = fqt_ref.shape[1]

    def load(h):
        n = s1_ref[few * width + h : few * width + h + 1]
        return fqt_ref[h], pair(g_ref, gg_ref, h, width), dl_ref[h], n

    def work(fqt, g, dl, n):
        norm = jnp.broadcast_to(n, (8, width))
        denom = dl + inside * dot_full(norm, fqt, NN)[:1]
        inv = 1.0 / denom
        return inv, dot_wide(fqt * (inv * head), g, NN)

    def store(h, inv, r):
        inv_ref[h] = inv
        r_ref[h] = r

    heads_loop(nh, load, work, store)


def fill_kernel(nh, at_ref, inv_ref, g_ref, gg_ref, v_ref, vg_ref, k_ref, kg_ref, w_ref,
                fk_ref, fkg_ref, pqt_ref, fqt_ref,
                mt_ref, cl_ref, gv_ref, sk_ref, sqt_ref):
    width = fqt_ref.shape[1]

    def load(h):
        return (at_ref[h], inv_ref[h], pair(g_ref, gg_ref, h, width), pair(v_ref, vg_ref, h, width),
                pair(k_ref, kg_ref, h, width), w_ref[h], both(fk_ref, fkg_ref, h, 0),
                pqt_ref[h], fqt_ref[h])

    def work(at, inv, g, v, k, w, fk, pqt, fqt):
        mt = dot(v, g, NT)
        cl = jnp.sum(at * mt, axis=0, keepdims=True)
        gv = dot_wide(at * inv, g, NN)
        return mt, cl, gv, jnp.exp(dot(k, w, NN) - fk), jnp.exp(pqt - fqt)

    def store(h, mt, cl, gv, sk, sqt):
        mt_ref[h] = mt
        cl_ref[h] = cl
        gv_ref[h] = gv
        sk_ref[h] = sk
        sqt_ref[h] = sqt

    heads_loop(nh, load, work, store)


def shift_kernel(nh, line_ref, s1_ref, s2_ref, cl_ref, inv_ref, g_ref, gg_ref, fqt_ref,
                 rn_ref, ut_ref, c_ref):
    width, rows = fqt_ref.shape[1:]
    inside, head = line_ref[:1], line_ref[1:2]
    few = nh - s2_ref.shape[0]

    def load(h):
        s = s1_ref[h * width : (h + 1) * width] if h < few else s2_ref[h - few]
        return s, cl_ref[h], inv_ref[h], pair(g_ref, gg_ref, h, width), fqt_ref[h]

    def work(s, cl, inv, g, fqt):
        ut = dot_wide(s, g, NT)
        c = (cl + inside * jnp.sum(fqt * ut, axis=0, keepdims=True)) * inv
        rn = dot_full(jnp.broadcast_to(-c * inv * head, (8, rows)), fqt, NT)[:1]
        return rn, ut, c

    def store(h, rn, ut, c):
        rn_ref[h] = rn
        ut_ref[h] = ut
        c_ref[h] = c

    heads_loop(nh, load, work, store)


def out_pair(x, own_ref, send_ref, h, width):
    half = x.shape[0] // 2
    own_ref[:, h * width : (h + 1) * width] = x[:half].astype(BF16)
    send_ref[:, h * width : (h + 1) * width] = x[half:]


def forward_kernel(nh, few, line_ref, keep_ref, ut_ref, c_ref, s1_ref, mt_ref, inv_ref, q_ref, qg_ref,
                   fqt_ref, sqt_ref, fkt_ref, fktg_ref, w_ref,
                   gq_ref, gqs_ref, qt_ref, gfk_ref):
    rows, width = gfk_ref.shape[1:]
    inside = line_ref[:1]

    def load(h):
        n = s1_ref[few * width + h : few * width + h + 1]
        return (ut_ref[h], c_ref[h], n, mt_ref[h], inv_ref[h], pair(q_ref, qg_ref, h, width),
                fqt_ref[h], sqt_ref[h], both(fkt_ref, fktg_ref, h, 1), w_ref[h])

    def work(ut, c, n, mt, inv, q, fqt, sqt, fkt, w):
        pt = (mt - c) * inv * keep_ref[...]
        gfk = dot_full(pt, fqt, NT)
        norm = jnp.broadcast_to(n, (width, width)).T
        carried = (ut - cat([norm] * (rows // width), 1) * c) * inv
        gpq = (dot_full(fkt, pt, NN) + inside * carried) * sqt
        hi, lo = split(gpq)
        gq = dot(cat([w, w], 1), cat([hi, lo], 0), NN).T
        qt = dot(cat([hi, lo], 1), cat([q, q], 0), NN).T
        return gq, qt, gfk

    def store(h, gq, qt, gfk):
        out_pair(gq, gq_ref, gqs_ref, h, width)
        qt_ref[h] = qt
        gfk_ref[h] = gfk

    heads_loop(nh, load, work, store)


def backward_kernel(nh, factor, later_ref, r_ref, rn_ref, gfk_ref, sk_ref, k_ref, kg_ref, v_ref, vg_ref,
                    qt_ref, hi_ref, lo_ref, *more_refs):
    *plane_refs, wt_ref = more_refs
    width = gfk_ref.shape[2]
    low, blocks, _ = plane_refs[0].shape
    chips = len(plane_refs)
    pieces = width // blocks

    def load(h):
        return (r_ref[h], rn_ref[h], gfk_ref[h], sk_ref[h], pair(k_ref, kg_ref, h, width),
                pair(v_ref, vg_ref, h, width), qt_ref[h])

    def work(r, rn, gfk, sk, k, v, qt):
        rh, rl = split(r)
        carried = dot(cat([v, v], 1), cat([rh, rl], 1), NT) + rn
        hi, lo = split((gfk + later_ref[...] * carried) * sk)
        return hi, lo, (dot(cat([k, k], 0), cat([hi, lo], 0), TN) + qt) * factor

    def store(h, hi, lo, wt):
        hi_ref[h] = hi
        lo_ref[h] = lo
        for p in range(pieces):
            wt_ref[h * pieces + p] = wt[p * blocks : (p + 1) * blocks]

    heads_loop(nh, load, work, store)
    chip = lax.axis_index("ctx") // 2
    for j, ref in enumerate(plane_refs):
        for z in range(low):
            ref[z] = wt_ref[z * chips + (chip ^ j)]


def rest_kernel(nh, later_ref, r_ref, hi_ref, lo_ref, gv0_ref, fk_ref, fkg_ref, w_ref,
                gk_ref, gks_ref, gv_ref, gvs_ref):
    width = hi_ref.shape[2]

    def load(h):
        return r_ref[h], hi_ref[h], lo_ref[h], gv0_ref[h], both(fk_ref, fkg_ref, h, 0), w_ref[h]

    def work(r, hi, lo, gv0, fk, w):
        gk = dot(cat([hi, lo], 1), cat([w, w], 1), NT)
        return gk, gv0 + later_ref[...] * dot_full(fk, r, NN)

    def store(h, gk, gv):
        out_pair(gk, gk_ref, gks_ref, h, width)
        out_pair(gv, gv_ref, gvs_ref, h, width)

    heads_loop(nh, load, work, store)


def fold_kernel(bit, parts, *refs):
    ins, outs = refs[:parts], refs[parts:]
    here = bit and bit()
    for i in range(outs[0].shape[0]):
        if bit is None:
            outs[0][i] = functools.reduce(jnp.add, [r[i] for r in ins])
        else:
            a = functools.reduce(jnp.add, [r[2 * i] for r in ins])
            b = functools.reduce(jnp.add, [r[2 * i + 1] for r in ins])
            outs[0][i] = jnp.where(here == 0, a, b)
            outs[1][i] = jnp.where(here == 0, b, a)


def corner_kernel(step, parts, *refs):
    ins, outs = refs[:parts], refs[parts:]
    bit, core = dp_bit(step), my_core()
    each = outs[0].shape[1]
    a, b = [functools.reduce(jnp.add, [r[i] for r in ins]) for i in range(2)]
    near, far = jnp.where(bit == 0, a, b), jnp.where(bit == 0, b, a)
    for x, mine_ref, other_ref in ((near, outs[0], outs[2]), (far, outs[1], outs[3])):
        mine_ref[0] = jnp.where(core == 0, x[:each], x[each:])
        other_ref[0] = jnp.where(core == 0, x[each:], x[:each])


def pick_kernel(step, a_ref, b_ref, c_ref, d_ref, keep_ref, send_ref):
    here = dp_bit(step) ^ my_core()
    own, got = a_ref[...] + b_ref[...], c_ref[...] + d_ref[...]
    keep_ref[...] = jnp.where(here == 0, own, got)
    send_ref[...] = jnp.where(here == 0, got, own)


def join_kernel(own_ref, got_ref, out_ref):
    core = my_core()
    half = own_ref.shape[1]
    out_ref[:, pl.ds(pl.multiple_of(core * half, half), half)] = own_ref[...]
    out_ref[:, pl.ds(pl.multiple_of((1 - core) * half, half), half)] = got_ref[...].astype(BF16)


def dp_bit(step):
    return (lax.axis_index("dp") // step) % 2


def call(kernel, outs, hbm=0, scratch=()):
    def run(*args):
        return pl.pallas_call(
            kernel,
            out_shape=[jax.ShapeDtypeStruct(s, d) for s, d in outs],
            in_specs=[pl.BlockSpec(memory_space=pltpu.HBM)] * hbm + [VM] * (len(args) - hbm),
            out_specs=[VM] * len(outs),
            scratch_shapes=list(scratch),
            compiler_params=pltpu.CompilerParams(vmem_limit_bytes=LIMIT),
        )(*args)

    return run


def shards(queries, keys, values, out_grad, feature_weight, doc_lengths):
    ctx = lax.axis_size("ctx")
    dp = lax.axis_size("dp")
    tok = queries.shape[1]
    heads, width, _ = feature_weight.shape
    ndoc = doc_lengths.shape[1]
    chips = ctx // 2
    nh = heads // 2
    rows = 2 * tok
    longest = ctx * tok // 4
    hops = -(-longest // rows)
    factor = 1.0 / math.sqrt(dp * ctx * tok)

    swap = [(i, i ^ 1) for i in range(ctx)]
    ahead = [(i, i + 2) for i in range(ctx - 2)]
    back = [(i + 2, i) for i in range(ctx - 2)]

    q, k, v, g = queries[0], keys[0], values[0], out_grad[0]
    w = feature_weight
    half = (tok, nh * width)

    def swapped(*arrays):
        return [lax.ppermute(x, "ctx", swap) for x in arrays]

    wide = (nh, rows, width)
    tall = (nh, width, rows)
    square = (nh, rows, rows)
    state = (nh, width, width)
    norm = (nh, 1, width)
    line = (nh, 1, rows)

    few = max(1, nh // 4)

    ins = [pltpu.with_memory_space_constraint(x, pltpu.HBM) for x in (k, v, q, g, w, doc_lengths)]
    ko, vo, qo, go, ks, vs, qs, gs, w, keep, lines, tail, later = call(
        functools.partial(cast_kernel, ndoc),
        [(half, BF16)] * 4 + [(half, F32)] * 4 + [((nh, width, width), BF16)]
        + [((rows, rows), F32), ((8, rows), F32), ((rows, width), F32), ((rows, width), F32)],
        len(ins),
        [pltpu.VMEM((4,) + half, BF16), pltpu.SMEM((1, ndoc), jnp.int32), pltpu.SemaphoreType.DMA((10,))],
    )(*ins)
    kg, vg = swapped(ks, vs)
    qg, gg = swapped(qs, gs)

    if hops > 1:
        ends = jnp.cumsum(doc_lengths[0])
        begins = jnp.concatenate([jnp.zeros((1,), jnp.int32), ends])

        chip = lax.axis_index("ctx") // 2

        def start_of(p):
            return jnp.max(jnp.where(begins <= p, begins, 0))

    def carry(x, forward):
        total = moved = lax.ppermute(x, "ctx", ahead if forward else back)
        for h in range(1, hops):
            moved = lax.ppermute(moved, "ctx", ahead if forward else back)
            if forward:
                gate = start_of(chip * rows) < (chip - h) * rows
            else:
                gate = start_of((chip + 1 + h) * rows) < (chip + 1) * rows
            total = total + jnp.where(gate, moved, 0.0)
        return total

    part = (nh, tok, width)
    flat = (nh, width, tok)
    fk, fkt, s_own, n_own = call(
        functools.partial(own_key_kernel, nh), [(part, F32), (flat, F32), (state, F32), (norm, F32)]
    )(ko, vo, w, lines, tail)
    fkg, fktg, s1, s2 = call(
        functools.partial(got_key_kernel, nh),
        [(part, F32), (flat, F32),
         ((few * width + -(-nh // 8) * 8, width), F32), ((nh - few, width, width), F32)],
    )(kg, vg, w, lines, tail, s_own, n_own)
    s1 = carry(s1, True)
    s2 = carry(s2, True)
    fqt, pqt, at, dl = call(
        functools.partial(query_kernel, nh), [(tall, F32), (tall, F32), (square, F32), (line, F32)]
    )(qo, qg, w, fk, fkg, keep)
    inv, r_loc = call(
        functools.partial(rstate_kernel, nh, few), [(line, F32), (state, F32)]
    )(lines, fqt, go, gg, dl, s1)
    r_in = carry(r_loc, False)
    mt, cl, gv0, sk, sqt = call(
        functools.partial(fill_kernel, nh),
        [(square, F32), (line, F32), (wide, F32), (wide, F32), (tall, F32)],
    )(at, inv, go, gg, vo, vg, ko, kg, w, fk, fkg, pqt, fqt)
    rn, ut, c = call(
        functools.partial(shift_kernel, nh), [(norm, F32), (tall, F32), (line, F32)]
    )(lines, s1, s2, cl, inv, go, gg, fqt)
    rn_in = carry(rn, False)
    gq, gqs, qt, gfk = call(
        functools.partial(forward_kernel, nh, few),
        [(half, BF16), (half, F32), (state, F32), (wide, F32)],
    )(lines, keep, ut, c, s1, mt, inv, qo, qg, fqt, sqt, fkt, fktg, w)

    def join(own, got):
        return call(join_kernel, [((tok, heads * width), BF16)])(own, got)[0][None]

    (gqg,) = swapped(gqs)
    out_q = join(gq, gqg)

    each = heads * width // (dp * ctx)
    low = dp // 2
    hi, lo, *planes = call(
        functools.partial(backward_kernel, nh, factor),
        [(wide, BF16)] * 2 + [((low, 2 * each, width), F32)] * chips,
        scratch=[pltpu.VMEM((low * chips, 2 * each, width), F32)],
    )(later, r_in, rn_in, gfk, sk, ko, kg, vo, vg, qt)
    gk, gks, gv, gvs = call(
        functools.partial(rest_kernel, nh), [(half, BF16), (half, F32), (half, BF16), (half, F32)]
    )(later, r_in, hi, lo, gv0, fk, fkg, w)

    moved = []
    for j in range(1, chips):
        perm = [(i, ((i // 2) ^ j) * 2 + i % 2) for i in range(ctx)]
        moved.append(lax.ppermute(planes[j], "ctx", perm))
    gkg, gvg = swapped(gks, gvs)
    out_k, out_v = join(gk, gkg), join(gv, gvg)

    def folded(parts, size, bit):
        return call(
            functools.partial(fold_kernel, bit, len(parts)),
            [(size, F32)] * (1 if bit is None else 2),
        )(*parts)

    def dp_moved(x, step, flip):
        perm = [(z * ctx + i, (z ^ step) * ctx + (i ^ flip)) for z in range(dp) for i in range(ctx)]
        return lax.ppermute(x, ("dp", "ctx"), perm)

    parts = [planes[0]] + moved
    left, step = low, 1
    while left > 2:
        left //= 2
        kept, sent = folded(parts, (left, 2 * each, width), functools.partial(dp_bit, step))
        parts = [kept, dp_moved(sent, step, 0)]
        step *= 2
    block = ((1, each, width), F32)
    kept, far, side, corner = call(
        functools.partial(corner_kernel, step, len(parts)), [block] * 4
    )(*parts)
    far = dp_moved(far, step, 0)
    corner = dp_moved(corner, step, 1)
    (side,) = swapped(side)
    step *= 2
    kept, sent = call(functools.partial(pick_kernel, step), [block] * 2)(kept, far, side, corner)
    (grad_weight,) = folded([kept, dp_moved(sent, step, 0)], block[0], None)
    return (out_q, out_k, out_v, grad_weight[0])


def solution(mesh):
    placed = (
        P("dp", "ctx", None),
        P("dp", "ctx", None),
        P("dp", "ctx", None),
        P("dp", "ctx", None),
        P(),
        P("dp", None),
    )
    return jax.shard_map(
        shards,
        mesh=mesh,
        in_specs=placed,
        out_specs=(
            P("dp", "ctx", None),
            P("dp", "ctx", None),
            P("dp", "ctx", None),
            P(("dp", "ctx"), None),
        ),
        check_vma=False,
    )
```
